32 devices in a mesh: dp: 8 (over z, x), tensor: 4 (over y, core).
Axes of the slice: x: 2, y: 2, z: 4, core: 2. Of those that a mesh axis runs over, the one named last changes fastest.
Arguments:
- tokens: bfloat16 [16384, 768], P(('dp', 'tensor')), may hold values from -6 to 6
- segments: int32 [16, 1024], P('dp'), may hold values from 0 to 23, never falling along the last dimension, each value on 1 to 512 neighbouring positions
- query_weight: float32 [768, 768], P('dp', 'tensor'), may hold values from -0.21875 to 0.21875
- query_bias: float32 [768], P('tensor'), may hold values from -1.5 to 1.5
- key_weight: float32 [768, 768], P('dp', 'tensor'), may hold values from -0.21875 to 0.21875
- value_weight: float32 [768, 768], P('dp', 'tensor'), may hold values from -0.21875 to 0.21875
- value_bias: float32 [768], P('tensor'), may hold values from -1.5 to 1.5
- out_weight: float32 [768, 768], P('dp', 'tensor'), may hold values from -1 to 1
- out_bias: float32 [768], replicated, may hold values from -1.5 to 1.5
- attn_gain: float32 [768], replicated, may hold values from 0.5 to 1.5
- attn_shift: float32 [768], replicated, may hold values from -1.5 to 1.5
- inner_weight: float32 [768, 3072], P('dp', 'tensor'), may hold values from -0.21875 to 0.21875
- inner_bias: float32 [3072], P('tensor'), may hold values from -1.5 to 1.5
- outer_weight: float32 [768, 3072], P('dp', 'tensor'), may hold values from -0.109375 to 0.109375
- outer_bias: float32 [768], replicated, may hold values from -1.5 to 1.5
- ffn_gain: float32 [768], replicated, may hold values from 0.5 to 1.5
- ffn_shift: float32 [768], replicated, may hold values from -1.5 to 1.5
- out_grad: bfloat16 [16384, 768], P(('dp', 'tensor')), may hold values from -6 to 6
Outputs:
- layer_out: bfloat16 [16384, 768], P(('dp', 'tensor'))
- tokens_grad: float32 [16384, 768], P(('dp', 'tensor'))
- query_weight_grad: float32 [768, 768], P('dp', 'tensor')
- query_bias_grad: float32 [768], P('tensor')
- key_weight_grad: float32 [768, 768], P('dp', 'tensor')
- value_weight_grad: float32 [768, 768], P('dp', 'tensor')
- value_bias_grad: float32 [768], P('tensor')
- out_weight_grad: float32 [768, 768], P('dp', 'tensor')
- out_bias_grad: float32 [768], replicated
- attn_gain_grad: float32 [768], replicated
- attn_shift_grad: float32 [768], replicated
- inner_weight_grad: float32 [768, 3072], P('dp', 'tensor')
- inner_bias_grad: float32 [3072], P('tensor')
- outer_weight_grad: float32 [768, 3072], P('dp', 'tensor')
- outer_bias_grad: float32 [768], replicated
- ffn_gain_grad: float32 [768], replicated
- ffn_shift_grad: float32 [768], replicated
The draws below stay inside these ranges and needn't reach their ends.
Inputs may be any that keep to these rules, and one draw needn't show every extreme that they name: `segments`: within each sequence the document ids never fall; a document spans 1 to 512 tokens, and some document spans exactly 512.
All inputs are finite; a program needn't handle non-finite values.
Results may differ from the reference program's by a relative error of at most 0.014.
The reference program's roundings to bfloat16 on the way count: a program that leaves them out, or rounds other values in their place, can miss the bound.
Values may be sent and summed in bfloat16 or wider, within the bound.
No kernel may reach another device: no remote copies, remote signals or barrier semaphores. Data moves between devices by JAX's collectives and lax.ppermute only.
A program may use at most 128 MiB of HBM per device.

```python
import math
import jax
import jax.numpy as jnp
import numpy as np
from jax import lax

D = 768
HEADS = 12
HD = 64
FF = 3072
LEN = 1024
DOCS = 24
MOST_DOC = 512
SEQS = 16
TOKENS = 16384


def block_scale(stream_key, extent, shards, least, high):
    loudness = 1.0
    for axis_at, parts in shards:
        heights = jax.random.uniform(jax.random.fold_in(jax.random.fold_in(stream_key, 6), axis_at), (parts,), jnp.float32, least / len(shards), high / len(shards))
        loudness = loudness * jnp.repeat(jnp.exp(heights), extent[axis_at] // parts).reshape((-1,) + (1,) * (len(extent) - 1 - axis_at))
    return loudness


def split_up(count, total, bound, skew):
    portions = [(1 << 20) // math.isqrt(grade ** skew) + 1 for grade in range(2, count + 1)]
    surplus, given = total - bound - (count - 1), [1] * (count - 1)
    while surplus > 0:
        candidates = [i for i in range(count - 1) if given[i] < bound]
        mass, left = sum([portions[i] for i in candidates]), surplus
        for i in candidates:
            extra = min(bound - given[i], max(1, left * portions[i] // mass), surplus)
            given[i] = given[i] + extra
            surplus = surplus - extra
    return np.array([bound] + given)


def ragged(own_key, amount, total, reach, skew):
    if amount == 2:
        one = jax.random.randint(own_key, (), max(1, total - reach), min(reach, total - 1) + 1)
        return jnp.stack([one, total - one])
    sizes = jnp.asarray(split_up(amount, total, reach, skew), jnp.int32)
    couples = (amount - 1) // 2
    giver, sink = sizes[1:1 + 2 * couples:2], sizes[2:2 + 2 * couples:2]
    slack = jnp.minimum(giver - 1, reach - sink)
    shifted = jax.random.randint(jax.random.fold_in(own_key, 1), (couples,), 0, 1 << 20) % (slack + 1)
    sizes = sizes.at[1:1 + 2 * couples:2].set(giver - shifted).at[2:2 + 2 * couples:2].set(sink + shifted)
    return sizes[jax.random.permutation(jax.random.fold_in(own_key, 2), amount)]


def bell_draw(rng, shape, width, reach, shards=(), dtype=jnp.bfloat16):
    gain = block_scale(rng, shape, shards, -0.22, 0.18) if shards else 1.0
    values = jax.random.normal(rng, shape, jnp.float32) * width * gain
    return jnp.minimum(jnp.maximum(values, -reach), reach).astype(dtype)


def setup_inputs(seed: int = 0) -> dict:
    splits = jax.random.split(jax.random.key(seed), 19)
    return {
        "tokens": bell_draw(splits[0], (TOKENS, D), 1.0, 6.0, ((0, 32),)),
        "segments": jax.vmap(lambda own: jnp.searchsorted(jnp.cumsum(ragged(own, DOCS, LEN, MOST_DOC, 2)), jnp.arange(LEN), side="right"))(jax.random.split(splits[1], SEQS)).reshape((SEQS, LEN)).astype(jnp.int32),
        "query_weight": bell_draw(splits[2], (D, D), D ** -0.5, 0.21875, ((0, 8), (1, 4)), jnp.float32),
        "query_bias": bell_draw(splits[3], (D,), 0.3, 1.5, ((0, 4),), jnp.float32),
        "key_weight": bell_draw(splits[4], (D, D), D ** -0.5, 0.21875, ((0, 8), (1, 4)), jnp.float32),
        "value_weight": bell_draw(splits[5], (D, D), D ** -0.5, 0.21875, ((0, 8), (1, 4)), jnp.float32),
        "value_bias": bell_draw(splits[6], (D,), 0.3, 1.5, ((0, 4),), jnp.float32),
        "out_weight": bell_draw(splits[7], (D, D), (D // 24) ** -0.5, 1.0, ((0, 8), (1, 4)), jnp.float32),
        "out_bias": bell_draw(splits[8], (D,), 0.3, 1.5, (), jnp.float32),
        "attn_gain": jnp.clip(1.0 + 0.1 * jax.random.normal(splits[9], (D,), jnp.float32), 0.5, 1.5),
        "attn_shift": bell_draw(splits[10], (D,), 0.3, 1.5, (), jnp.float32),
        "inner_weight": bell_draw(splits[11], (D, FF), D ** -0.5, 0.21875, ((0, 8), (1, 4)), jnp.float32),
        "inner_bias": bell_draw(splits[12], (FF,), 0.3, 1.5, ((0, 4),), jnp.float32),
        "outer_weight": bell_draw(splits[13], (D, FF), FF ** -0.5, 0.109375, ((0, 8), (1, 4)), jnp.float32),
        "outer_bias": bell_draw(splits[14], (D,), 0.3, 1.5, (), jnp.float32),
        "ffn_gain": jnp.clip(1.0 + 0.1 * jax.random.normal(splits[15], (D,), jnp.float32), 0.5, 1.5),
        "ffn_shift": bell_draw(splits[16], (D,), 0.3, 1.5, (), jnp.float32),
        "out_grad": bell_draw(splits[17], (TOKENS, D), 1.0, 6.0, ((0, 32),)),
    }


@jax.custom_vjp
def low(v):
    return lax.optimization_barrier(v.astype(jnp.bfloat16)).astype(jnp.float32)

@jax.custom_vjp
def low_back(v):
    return v

def low_keep(v):
    return (low(v), None)

def low_pass(kept, grad):
    return (grad,)

def back_keep(v):
    return (v, None)

def back_low(kept, grad):
    return (low(grad),)
low.defvjp(low_keep, low_pass)
low_back.defvjp(back_keep, back_low)
HIGH = lax.Precision.HIGHEST

def matmul(left_mat, right_mat):
    return jnp.dot(left_mat, right_mat, precision=HIGH, preferred_element_type=jnp.float32)

def normalize(residual, norm_gain, norm_shift):
    mean_val = lax.optimization_barrier(jnp.mean(residual, axis=-1, keepdims=True))
    center = residual - mean_val
    spread = lax.optimization_barrier(jnp.mean(center * center, axis=-1, keepdims=True))
    return center * lax.rsqrt(spread + 1e-06) * norm_gain + norm_shift

def attend_one(scan_item):
    queries, key_rows, value_rows, segment = scan_item
    scores = jnp.einsum('qhd,khd->hqk', queries, key_rows, precision=HIGH)
    scores = low_back(scores * (1.0 / math.sqrt(HD)))
    same_doc = segment[:, None] == segment[None, :]
    scores = jnp.where(same_doc[None, :, :], scores, -1e+30)
    row_max = lax.optimization_barrier(jnp.max(scores, axis=-1, keepdims=True))
    exp_scores = jnp.exp(scores - row_max)
    probs = low(exp_scores / lax.optimization_barrier(jnp.sum(exp_scores, axis=-1, keepdims=True)))
    mixed_heads = jnp.einsum('hqk,khd->qhd', probs, value_rows, precision=HIGH)
    return low(low_back(mixed_heads)).reshape(queries.shape[0], HEADS * HD)

def forward(tok_rows, seg_rows, params):
    query_weight, query_bias, key_weight, value_weight, value_bias, out_weight, out_bias, attn_gain, attn_shift, inner_weight, inner_bias, outer_weight, outer_bias, ffn_gain, ffn_shift = params
    query_all = low(low_back(matmul(tok_rows, low(query_weight))) + query_bias)
    key_all = low(low_back(matmul(tok_rows, low(key_weight))))
    value_all = low(low_back(matmul(tok_rows, low(value_weight))) + value_bias)
    seq_count = seg_rows.shape[0]

    def heads_view(flat_array):
        return flat_array.reshape(seq_count, LEN, HEADS, HD)
    mixed_all = lax.map(jax.checkpoint(attend_one), (heads_view(query_all), heads_view(key_all), heads_view(value_all), seg_rows))
    mixed_all = mixed_all.reshape(seq_count * LEN, D)
    attn_out = low_back(matmul(mixed_all, low(out_weight).T))
    hidden = normalize(tok_rows + attn_out + out_bias, attn_gain, attn_shift)
    inner_pre = low_back(matmul(low(hidden), low(inner_weight))) + inner_bias
    active = low(jax.nn.gelu(inner_pre, approximate=False))
    ffn_out = low_back(matmul(active, low(outer_weight).T))
    return normalize(hidden + ffn_out + outer_bias, ffn_gain, ffn_shift)

def reference(tokens, segments, query_weight, query_bias, key_weight, value_weight, value_bias, out_weight, out_bias, attn_gain, attn_shift, inner_weight, inner_bias, outer_weight, outer_bias, ffn_gain, ffn_shift, out_grad):
    params = (query_weight, query_bias, key_weight, value_weight, value_bias, out_weight, out_bias, attn_gain, attn_shift, inner_weight, inner_bias, outer_weight, outer_bias, ffn_gain, ffn_shift)
    seq_group = math.gcd(SEQS, max(1, 4096 // LEN))
    rounds = SEQS // seq_group
    tok_all = tokens.astype(jnp.float32).reshape(rounds, seq_group * LEN, D)
    cot_all = out_grad.astype(jnp.float32).reshape(rounds, seq_group * LEN, D)
    seg_all = segments.reshape(rounds, seq_group, LEN)
    totals = jax.tree.map(jnp.zeros_like, params)

    def one_round(carried, scan_item):
        tok_rows, seg_rows, cotangent = scan_item

        def run_group(rows_in, params_in):
            return forward(rows_in, seg_rows, params_in)
        result, pull_back = jax.vjp(run_group, tok_rows, params)
        rows_grad, params_grad = pull_back(cotangent)
        carried = jax.tree.map(jnp.add, carried, params_grad)
        return (carried, (result.astype(jnp.bfloat16), rows_grad))
    totals, (outputs, grads) = lax.scan(one_round, totals, (tok_all, seg_all, cot_all))
    layer_out = outputs.reshape(TOKENS, D)
    tokens_grad = grads.reshape(TOKENS, D)
    return (layer_out, tokens_grad, totals[0], totals[1], totals[2], totals[3], totals[4], totals[5], totals[6], totals[7], totals[8], totals[9], totals[10], totals[11], totals[12], totals[13], totals[14])
```

```python
import math

import jax
import jax.numpy as jnp
from jax import lax
from jax.sharding import Mesh
from jax.sharding import PartitionSpec as P

HD = 64
NEG_FILL = -1e30
ROOT_HALF = 0.7071067811865476
INV_ROOT_TAU = 0.3989422804014327
bf16 = jnp.bfloat16
f32 = jnp.float32


def normalize_rows(residual, norm_gain, norm_shift):
    center = residual - jnp.mean(residual, axis=-1, keepdims=True)
    inv_spread = lax.rsqrt(jnp.mean(center * center, axis=-1, keepdims=True) + 1e-06)
    normed = center * inv_spread
    return (normed * norm_gain + norm_shift, normed, inv_spread)


def normalize_back(upstream, normed, inv_spread, norm_gain):
    scaled = upstream * norm_gain
    inner_term = (
        scaled
        - jnp.mean(scaled, axis=-1, keepdims=True)
        - normed * jnp.mean(scaled * normed, axis=-1, keepdims=True)
    )
    return (inv_spread * inner_term, jnp.sum(upstream * normed, axis=0), jnp.sum(upstream, axis=0))


def phi_cdf(pre_act):
    return 0.5 * (1.0 + lax.erf(pre_act * ROOT_HALF))


def mm(left, right):
    return jnp.dot(left, right, preferred_element_type=f32)


def mm_nt(left, right):
    return lax.dot_general(left, right, (((1,), (1,)), ((), ())), preferred_element_type=f32)


def mm_tn(left, right):
    return lax.dot_general(left, right, (((0,), (0,)), ((), ())), preferred_element_type=f32)


def swap(value, axis):
    return lax.ppermute(value, axis, [(0, 1), (1, 0)])


def shift(value, axis, steps):
    size = lax.axis_size(axis)
    return lax.ppermute(value, axis, [(i, (i + steps) % size) for i in range(size)])


def pick(value, index, axis):
    return lax.dynamic_index_in_dim(value, index, axis, keepdims=False)


def gather_line(block):
    size = lax.axis_size("z")
    if size > 4:
        return lax.all_gather(block, "z", axis=0)
    place = lax.axis_index("z")
    out = jnp.zeros((size, *block.shape), block.dtype)
    out = lax.dynamic_update_index_in_dim(out, block, place, 0)
    for k in range(1, size):
        out = lax.dynamic_update_index_in_dim(
            out, shift(block, "z", k), lax.rem(place + size - k, size), 0
        )
    return out


def weave(same, other, x):
    first = jnp.where(x == 0, same, other)
    second = jnp.where(x == 0, other, same)
    both = jnp.stack([first, second], axis=1)
    return both.reshape(-1, both.shape[-1])


def spread(block):
    x = lax.axis_index("x")
    line = gather_line(block)
    half = line.shape[0] // 2
    low, high = line[:half], line[half:]
    low_x, high_y = swap(low, "x"), swap(high, "y")
    low_two = swap(jnp.stack([low, low_x]), "y")
    high_two = swap(jnp.stack([high, high_y]), "x")
    own = weave(jnp.concatenate([low, high]), jnp.concatenate([low_x, high_two[0]]), x)
    far = weave(jnp.concatenate([low_two[0], high_y]), jnp.concatenate([low_two[1], high_two[1]]), x)
    return own, far


def collect(own, far, rows):
    x, z = lax.axis_index("x"), lax.axis_index("z")
    size = lax.axis_size("z")
    half = size // 2
    cols = own.shape[1]
    own = own.reshape(size, 2, rows, cols)
    far = far.reshape(size, 2, rows, cols)
    got = swap(
        jnp.stack([pick(own[:half], 1 - x, 1), pick(far[:half], 1 - x, 1)]).astype(bf16), "x"
    ).astype(f32)
    low = pick(own[:half], x, 1) + got[0]
    low_far = pick(far[:half], x, 1) + got[1]
    low = low + swap(low_far.astype(bf16), "y").astype(f32)
    high = own[half:] + swap(far[half:].astype(bf16), "y").astype(f32)
    high = pick(high, x, 1) + swap(pick(high, 1 - x, 1).astype(bf16), "x").astype(f32)
    line = jnp.concatenate([low, high])
    if size > 4:
        return lax.psum_scatter(line, "z", scatter_dimension=0)
    total = pick(line, z, 0)
    for k in range(1, size):
        total = total + shift(pick(line, lax.rem(z + k, size), 0).astype(bf16), "z", k).astype(f32)
    return total


def total_small(value):
    value = value + swap(value, "x")
    value = value + swap(value, "y")
    size = lax.axis_size("z")
    if size > 4:
        return lax.psum(value, "z")
    total = value
    for k in range(1, size):
        total = total + shift(value, "z", k)
    return total


def masked_scores(queries, key_rows, seg_rows, seg_cols):
    scores = jnp.einsum("qhd,khd->hqk", queries, key_rows, preferred_element_type=f32)
    same_doc = seg_rows[:, None] == seg_cols[None, :]
    return jnp.where(same_doc[None, :, :], scores * (1.0 / math.sqrt(HD)), NEG_FILL)


def attend_forward(queries, key_rows, value_rows, segment):
    scores = masked_scores(queries, key_rows, segment, segment)
    row_max = jnp.max(scores, axis=-1, keepdims=True)
    exp_scores = jnp.exp(scores - row_max)
    row_total = jnp.sum(exp_scores, axis=-1, keepdims=True)
    prob_low = (exp_scores / row_total).astype(bf16)
    mixed = jnp.einsum("hqk,khd->qhd", prob_low, value_rows, preferred_element_type=f32)
    return mixed.astype(bf16), row_max + jnp.log(row_total)


def attend_back(queries, key_rows, value_rows, segment, log_rows, grad_rows):
    scale = 1.0 / math.sqrt(HD)
    scores = masked_scores(queries, key_rows, segment, segment)
    probs = jnp.exp(scores - log_rows)
    prob_low = probs.astype(bf16)
    value_grad = jnp.einsum("hqk,qhd->khd", prob_low, grad_rows, preferred_element_type=f32)
    prob_grad = jnp.einsum("qhd,khd->hqk", grad_rows, value_rows, preferred_element_type=f32)
    row_dot = jnp.sum(probs * prob_grad, axis=-1, keepdims=True)
    score_low = (probs * (prob_grad - row_dot)).astype(bf16)
    query_grad = jnp.einsum("hqk,khd->qhd", score_low, key_rows, preferred_element_type=f32) * scale
    key_grad = jnp.einsum("hqk,qhd->khd", score_low, queries, preferred_element_type=f32) * scale
    return query_grad, key_grad, value_grad


def shards(
    tokens,
    segments,
    query_weight,
    query_bias,
    key_weight,
    value_weight,
    value_bias,
    out_weight,
    out_bias,
    attn_gain,
    attn_shift,
    inner_weight,
    inner_bias,
    outer_weight,
    outer_bias,
    ffn_gain,
    ffn_shift,
    out_grad,
):
    share, width = tokens.shape
    rows, head_width = query_weight.shape
    units = inner_weight.shape[1]
    length = segments.shape[1]
    y, core = lax.axis_index("y"), lax.axis_index("c")
    start = core * share
    other_start = (1 - core) * share

    def own_rows(full):
        return lax.dynamic_slice_in_dim(full, start, share, 0)

    def other_rows(full):
        return lax.dynamic_slice_in_dim(full, other_start, share, 0)

    def whole(own):
        other = swap(own, "c")
        return jnp.where(core == 0, jnp.concatenate([own, other]), jnp.concatenate([other, own]))

    def pair_sum(product):
        sent = swap(product(other_rows).astype(bf16), "c")
        return product(own_rows) + sent.astype(f32)

    segment = pick(segments, y, 0)
    biases = jnp.concatenate([query_bias, value_bias, inner_bias])
    far_biases = swap(biases, "y")
    head_weights = jnp.concatenate(
        [query_weight, key_weight, value_weight, out_weight], axis=1
    ).astype(bf16)
    full_tokens = whole(tokens)
    head_own, head_far = spread(head_weights)
    inner_own, inner_far = spread(inner_weight.astype(bf16))
    outer_own, outer_far = spread(outer_weight.astype(bf16))

    def columns(part):
        at = slice(part * head_width, (part + 1) * head_width)
        return jnp.concatenate([head_own[:, at], head_far[:, at]], axis=1)

    query_mat, key_mat, value_mat, out_mat = (columns(part) for part in range(4))
    two_query_bias = jnp.concatenate([biases[:head_width], far_biases[:head_width]])
    two_value_bias = jnp.concatenate(
        [biases[head_width : 2 * head_width], far_biases[head_width : 2 * head_width]]
    )
    inner_mat = jnp.concatenate([inner_own, inner_far], axis=1)
    outer_mat = jnp.concatenate([outer_own, outer_far], axis=1)
    two_inner_bias = jnp.concatenate([biases[2 * head_width :], far_biases[2 * head_width :]])

    query_low = (mm(full_tokens, query_mat) + two_query_bias).astype(bf16)
    key_low = mm(full_tokens, key_mat).astype(bf16)
    value_low = (mm(full_tokens, value_mat) + two_value_bias).astype(bf16)

    def heads_view(flat):
        return flat.reshape(length, -1, HD)

    mixed_heads, log_totals = attend_forward(
        heads_view(query_low), heads_view(key_low), heads_view(value_low), segment
    )
    mixed = mixed_heads.reshape(length, -1)
    attn_total = pair_sum(lambda take: mm_nt(take(mixed), out_mat))
    hidden, normed_one, inv_one = normalize_rows(
        tokens.astype(f32) + attn_total + out_bias, attn_gain, attn_shift
    )
    hidden_low = whole(hidden.astype(bf16))
    inner_pre = mm(hidden_low, inner_mat) + two_inner_bias
    cdf = phi_cdf(inner_pre)
    active_low = (inner_pre * cdf).astype(bf16)
    slope = cdf + inner_pre * jnp.exp(-0.5 * inner_pre * inner_pre) * INV_ROOT_TAU
    ffn_total = pair_sum(lambda take: mm_nt(take(active_low), outer_mat))
    out_full, normed_two, inv_two = normalize_rows(
        hidden + ffn_total + outer_bias, ffn_gain, ffn_shift
    )
    layer_out = out_full.astype(bf16)
    grad_two, ffn_gain_part, ffn_shift_part = normalize_back(
        out_grad.astype(f32), normed_two, inv_two, ffn_gain
    )
    grad_two_low = whole(grad_two.astype(bf16))
    outer_grad_own = mm_tn(grad_two_low, active_low[:, :units])
    outer_grad_far = mm_tn(grad_two_low, active_low[:, units:])
    outer_sum = collect(outer_grad_own, outer_grad_far, rows)
    inner_grad = mm(grad_two_low, outer_mat) * slope
    inner_bias_part = jnp.sum(inner_grad, axis=0)
    inner_low = inner_grad.astype(bf16)
    inner_grad_own = mm_tn(hidden_low, inner_low[:, :units])
    inner_grad_far = mm_tn(hidden_low, inner_low[:, units:])
    inner_sum = collect(inner_grad_own, inner_grad_far, rows)
    back_total = pair_sum(lambda take: mm_nt(take(inner_low), inner_mat))
    grad_one, attn_gain_part, attn_shift_part = normalize_back(
        grad_two + back_total, normed_one, inv_one, attn_gain
    )
    grad_one_low = whole(grad_one.astype(bf16))
    out_w_grad = mm_tn(grad_one_low, mixed)
    mixed_grad = mm(grad_one_low, out_mat).astype(bf16)
    query_grad, key_grad, value_grad = attend_back(
        heads_view(query_low),
        heads_view(key_low),
        heads_view(value_low),
        segment,
        log_totals,
        heads_view(mixed_grad),
    )
    query_grad, key_grad, value_grad = (
        grad.reshape(length, -1) for grad in (query_grad, key_grad, value_grad)
    )
    query_bias_part = jnp.sum(query_grad, axis=0)
    value_bias_part = jnp.sum(value_grad, axis=0)
    query_grad, key_grad, value_grad = (
        grad.astype(bf16) for grad in (query_grad, key_grad, value_grad)
    )
    head_grads = (
        mm_tn(full_tokens, query_grad),
        mm_tn(full_tokens, key_grad),
        mm_tn(full_tokens, value_grad),
        out_w_grad,
    )
    head_sum = collect(
        jnp.concatenate([grad[:, :head_width] for grad in head_grads], axis=1),
        jnp.concatenate([grad[:, head_width:] for grad in head_grads], axis=1),
        rows,
    )
    input_total = pair_sum(
        lambda take: mm_nt(take(query_grad), query_mat)
        + mm_nt(take(key_grad), key_mat)
        + mm_nt(take(value_grad), value_mat)
    )
    tokens_grad = grad_one + input_total
    row_sums = jnp.concatenate(
        [
            jnp.sum(grad_one, axis=0),
            attn_gain_part,
            attn_shift_part,
            jnp.sum(grad_two, axis=0),
            ffn_gain_part,
            ffn_shift_part,
        ]
    )
    row_sums = row_sums + swap(row_sums, "c")

    def in_order(part, size):
        own, far = part[:size], part[size:]
        return jnp.where(y == 0, jnp.concatenate([own, far]), jnp.concatenate([far, own]))

    sums = total_small(
        jnp.concatenate(
            [
                row_sums,
                in_order(query_bias_part, head_width),
                in_order(value_bias_part, head_width),
                in_order(inner_bias_part, units),
            ]
        )
    )
    out_bsum, attn_gsum, attn_ssum, outer_bsum, ffn_gsum, ffn_ssum = (
        sums[i * width : (i + 1) * width] for i in range(6)
    )
    at = 6 * width

    def own_part(begin, size):
        return lax.dynamic_slice_in_dim(sums[begin : begin + 2 * size], y * size, size, 0)

    query_bias_grad = own_part(at, head_width)
    value_bias_grad = own_part(at + 2 * head_width, head_width)
    inner_bias_grad = own_part(at + 4 * head_width, units)
    query_wsum, key_wsum, value_wsum, out_wsum = (
        head_sum[:, part * head_width : (part + 1) * head_width] for part in range(4)
    )
    return (
        layer_out,
        tokens_grad,
        query_wsum,
        query_bias_grad,
        key_wsum,
        value_wsum,
        value_bias_grad,
        out_wsum,
        out_bsum,
        attn_gsum,
        attn_ssum,
        inner_sum,
        inner_bias_grad,
        outer_sum,
        outer_bsum,
        ffn_gsum,
        ffn_ssum,
    )


def solution(mesh):
    groups, tensor = mesh.shape["dp"], mesh.shape["tensor"]
    grid = Mesh(mesh.devices.reshape(groups // 2, 2, tensor // 2, 2), ("z", "x", "y", "c"))
    dp, tp = ("z", "x"), ("y", "c")
    every = ("z", "x", "y", "c")
    in_specs = (
        P(every, None),
        P(dp, None),
        P(dp, tp),
        P(tp),
        P(dp, tp),
        P(dp, tp),
        P(tp),
        P(dp, tp),
        P(),
        P(),
        P(),
        P(dp, tp),
        P(tp),
        P(dp, tp),
        P(),
        P(),
        P(),
        P(every, None),
    )
    out_specs = (
        P(every, None),
        P(every, None),
        P(dp, tp),
        P(tp),
        P(dp, tp),
        P(dp, tp),
        P(tp),
        P(dp, tp),
        P(),
        P(),
        P(),
        P(dp, tp),
        P(tp),
        P(dp, tp),
        P(),
        P(),
        P(),
    )
    return jax.shard_map(shards, mesh=grid, in_specs=in_specs, out_specs=out_specs, check_vma=False)
```

```python
import functools

import jax
import jax.numpy as jnp
from jax import lax
from jax.experimental import pallas as pl
from jax.experimental.pallas import tpu as pltpu
from jax.sharding import Mesh
from jax.sharding import PartitionSpec as P

HD = 64
TILE = 128
SCALE = 0.125
NEG_FILL = -1e30
ROOT_HALF = 0.7071067811865476
INV_ROOT_TAU = 0.3989422804014327
bf16 = jnp.bfloat16
f32 = jnp.float32

HEADS = ((0, 1, 0, 2, 0, 0), (0, 1, 1, 2, 1, 0), (4, 5, 0, 4, 1, 1))


def normalize_rows(residual, norm_gain, norm_shift):
    center = residual - jnp.mean(residual, axis=-1, keepdims=True)
    inv_spread = lax.rsqrt(jnp.mean(center * center, axis=-1, keepdims=True) + 1e-06)
    normed = center * inv_spread
    return (normed * norm_gain + norm_shift, normed, inv_spread)


def normalize_back(upstream, normed, inv_spread, norm_gain):
    scaled = upstream * norm_gain
    inner_term = (
        scaled
        - jnp.mean(scaled, axis=-1, keepdims=True)
        - normed * jnp.mean(scaled * normed, axis=-1, keepdims=True)
    )
    return (inv_spread * inner_term, jnp.sum(upstream * normed, axis=0), jnp.sum(upstream, axis=0))


def phi_cdf(pre_act):
    return 0.5 * (1.0 + lax.erf(pre_act * ROOT_HALF))


def mm(left, right):
    return lax.dot_general(left, right, (((1,), (0,)), ((), ())), preferred_element_type=f32)


def mm_nt(left, right):
    return lax.dot_general(left, right, (((1,), (1,)), ((), ())), preferred_element_type=f32)


def mm_tn(left, right):
    return lax.dot_general(left, right, (((0,), (0,)), ((), ())), preferred_element_type=f32)


def after(value, *earlier):
    return lax.optimization_barrier((value, *earlier))[0]


def swap(value, axis):
    return lax.ppermute(value, axis, [(0, 1), (1, 0)])


def shift(value, axis, steps):
    size = lax.axis_size(axis)
    return lax.ppermute(value, axis, [(i, (i + steps) % size) for i in range(size)])


def pick(value, index, axis):
    return lax.dynamic_index_in_dim(value, index, axis, keepdims=False)


def line_parts(block):
    size = lax.axis_size("z")
    if size > 4:
        return (lax.all_gather(block, "z", axis=0),)
    return (block, *(shift(block, "z", k) for k in range(1, size)))


def line_order(parts):
    size = lax.axis_size("z")
    if size > 4:
        return parts[0]
    place = lax.axis_index("z")
    out = jnp.zeros((size, *parts[0].shape), parts[0].dtype)
    for k, part in enumerate(parts):
        out = lax.dynamic_update_index_in_dim(out, part, lax.rem(place + size - k, size), 0)
    return out


def all_after(values, *earlier):
    return [after(value, *earlier) for value in values]


def spread_first(line):
    half = line.shape[0] // 2
    low, high = line[:half], line[half:]
    return low, high, swap(low, "x"), swap(high, "y")


def spread_second(low, high, low_x, high_y):
    return swap(jnp.stack([low, low_x]), "y"), swap(jnp.stack([high, high_y]), "x")


def in_order(index, same, other, axis):
    first = jnp.where(index == 0, same, other)
    second = jnp.where(index == 0, other, same)
    return jnp.stack([first, second], axis=axis)


def weave(same, other, x):
    both = in_order(x, same, other, 1)
    return both.reshape(-1, both.shape[-1])


def spread_end(low, high, low_x, high_y, low_two, high_two):
    x = lax.axis_index("x")
    own = weave(jnp.concatenate([low, high]), jnp.concatenate([low_x, high_two[0]]), x)
    far = weave(jnp.concatenate([low_two[0], high_y]), jnp.concatenate([low_two[1], high_two[1]]), x)
    return own, far


def plane_end(line):
    cols = line.shape[-1]
    return line[:, 0].reshape(-1, cols), line[:, 1].reshape(-1, cols)


def collect_first(own, far, rows):
    x = lax.axis_index("x")
    size = lax.axis_size("z")
    half = size // 2
    cols = own.shape[1]
    own = own.reshape(size, 2, rows, cols)
    far = far.reshape(size, 2, rows, cols)
    low_got = swap(
        jnp.stack([pick(own[:half], 1 - x, 1), pick(far[:half], 1 - x, 1)]).astype(bf16), "x"
    )
    high_got = swap(far[half:].astype(bf16), "y")
    return own, far, low_got, high_got


def collect_second(own, far, low_got, high_got):
    x = lax.axis_index("x")
    half = own.shape[0] // 2
    low = pick(own[:half], x, 1) + low_got[0].astype(f32)
    low_far = pick(far[:half], x, 1) + low_got[1].astype(f32)
    high = pick(own[half:], x, 1) + pick(high_got, x, 1).astype(f32)
    high_far = pick(own[half:], 1 - x, 1) + pick(high_got, 1 - x, 1).astype(f32)
    return low, high, swap(low_far.astype(bf16), "y"), swap(high_far.astype(bf16), "x")


def collect_third(low, high, low_got, high_got):
    return jnp.concatenate([low + low_got.astype(f32), high + high_got.astype(f32)])


def line_sum(line):
    z = lax.axis_index("z")
    size = lax.axis_size("z")
    if size > 4:
        return (lax.psum_scatter(line, "z", scatter_dimension=0),)
    sent = [
        shift(pick(line, lax.rem(z + k, size), 0).astype(bf16), "z", k) for k in range(1, size)
    ]
    return (pick(line, z, 0), *sent)


def add_all(parts):
    total = parts[0]
    for part in parts[1:]:
        total = total + part.astype(f32)
    return total


def split_low(rows):
    first = rows.astype(bf16)
    return jnp.concatenate([first, (rows - first.astype(f32)).astype(bf16)])


def join_low(pairs):
    half = pairs.shape[0] // 2
    return pairs[:half].astype(f32) + pairs[half:].astype(f32)


def tile(index):
    return slice(index * TILE, (index + 1) * TILE)


def keep_half(value, half):
    lane = lax.broadcasted_iota(jnp.int32, value.shape, 1)
    keep = lane < HD if half == 0 else lane >= HD
    return jnp.where(keep, value, jnp.zeros_like(value))


def fold(value, how):
    out = value[:8]
    for at in range(8, value.shape[0], 8):
        out = how(out, value[at : at + 8])
    return out


def document_bias(seg_col, seg_row, at, block):
    same = seg_col[pl.ds(at, block), :] == seg_row[:, :]
    return jnp.where(same, 0.0, NEG_FILL)


def attend_forward_kernel(
    groups, block, bounds, *refs
):
    projs, (seg_col, seg_row) = refs[:groups], refs[groups : groups + 2]
    mixes, lse_ref = refs[groups + 2 : 2 * groups + 2], refs[2 * groups + 2]
    score, top, total, acc, query = refs[2 * groups + 3 :]
    step = pl.program_id(0)
    rows = mixes[0].shape[0]
    low, high = bounds[0, step], bounds[1, step]
    here = pl.ds(pl.multiple_of(step * rows, rows), rows)
    heads = [(projs[g], *spec) for g in range(groups) for spec in HEADS]
    for h, (proj, qt, _, qh, _, _, _) in enumerate(heads):
        query[h] = keep_half(proj[here, tile(qt)] * SCALE, qh)
    top[...] = jnp.full_like(top, NEG_FILL)
    total[...] = jnp.zeros_like(total)
    acc[...] = jnp.zeros_like(acc)

    def scores(kb, carry):
        at = pl.multiple_of(kb * block, block)
        bias = document_bias(seg_col, seg_row, at, block)
        for h, (proj, _, kt, _, _, _, _) in enumerate(heads):
            value = mm_nt(proj[pl.ds(at, block), tile(kt)], query[h]) + bias
            score[h, pl.ds(at, block), :] = value
            top[h] = jnp.maximum(top[h], fold(value, jnp.maximum))
        return carry

    lax.fori_loop(low, high, scores, 0)
    row_max = [jnp.max(top[h], axis=0, keepdims=True) for h in range(len(heads))]

    def mix(kb, carry):
        at = pl.multiple_of(kb * block, block)
        for h, (proj, _, _, _, vt, _, _) in enumerate(heads):
            value = jnp.exp(score[h, pl.ds(at, block), :] - row_max[h])
            total[h] = total[h] + fold(value, jnp.add)
            acc[h] = acc[h] + mm_tn(proj[pl.ds(at, block), tile(vt)], value.astype(bf16))
        return carry

    lax.fori_loop(low, high, mix, 0)
    for g in range(groups):
        parts = []
        for h in range(3 * g, 3 * g + 3):
            half = heads[h][5]
            row_sum = jnp.sum(total[h], axis=0, keepdims=True)
            lse_ref[8 * g + h - 3 * g : 8 * g + h - 3 * g + 1, :] = row_max[h] + jnp.log(row_sum)
            parts.append(acc[h, half * HD : (half + 1) * HD, :] / row_sum)
        parts.insert(2, jnp.zeros_like(parts[0]))
        for pair in range(2):
            both = jnp.concatenate(parts[2 * pair : 2 * pair + 2], axis=0)
            mixes[g][:, tile(pair)] = both.T.astype(bf16)


def document_blocks(segment, rows, block):
    first, last = segment[::rows], segment[rows - 1 :: rows]
    low = jnp.sum((segment[None, :] < first[:, None]).astype(jnp.int32), axis=1)
    high = jnp.sum((segment[None, :] <= last[:, None]).astype(jnp.int32), axis=1)
    return jnp.stack([low // block, (high + block - 1) // block])


def attend_forward(projs, segment, rows=512, block=256):
    length, cols = projs[0].shape
    groups = len(projs)
    count = 3 * groups
    whole = lambda width: pl.BlockSpec((length, width), lambda i, b: (0, 0))
    part = lambda width: pl.BlockSpec((rows, width), lambda i, b: (i, 0))
    outs = pl.pallas_call(
        functools.partial(attend_forward_kernel, groups, block),
        grid_spec=pltpu.PrefetchScalarGridSpec(
            num_scalar_prefetch=1,
            grid=(length // rows,),
            in_specs=[whole(cols)] * groups
            + [whole(1), pl.BlockSpec((1, rows), lambda i, b: (0, i))],
            out_specs=[part(2 * TILE)] * groups
            + [pl.BlockSpec((8 * groups, rows), lambda i, b: (0, i))],
            scratch_shapes=[
                pltpu.VMEM((count, length, rows), f32),
                pltpu.VMEM((count, 8, rows), f32),
                pltpu.VMEM((count, 8, rows), f32),
                pltpu.VMEM((count, TILE, rows), f32),
                pltpu.VMEM((count, rows, TILE), bf16),
            ],
        ),
        out_shape=[jax.ShapeDtypeStruct((length, 2 * TILE), bf16)] * groups
        + [jax.ShapeDtypeStruct((8 * groups, length), f32)],
        compiler_params=pltpu.CompilerParams(vmem_limit_bytes=48 << 20),
        cost_estimate=pl.CostEstimate(
            flops=1_000_000_000, transcendentals=length * length * 3, bytes_accessed=8 << 20
        ),
        name="attend_forward",
    )(document_blocks(segment, rows, block), *projs, segment[:, None], segment[None, :])
    return outs[:groups], outs[groups]


def attend_back_kernel(
    block,
    bounds,
    proj,
    seg_col,
    seg_row,
    mixed,
    lse,
    mixed_grad,
    grad_ref,
    bias_ref,
    grad_acc,
    query_acc,
    query,
    upstream,
    row_dot,
):
    step = pl.program_id(0)
    rows = mixed.shape[0]
    low, high = bounds[0, step], bounds[1, step]
    here = pl.ds(pl.multiple_of(step * rows, rows), rows)

    @pl.when(step == 0)
    def _():
        grad_acc[...] = jnp.zeros_like(grad_acc)
        bias_ref[...] = jnp.zeros_like(bias_ref)

    query_acc[...] = jnp.zeros_like(query_acc)
    for h, (qt, _, qh, _, vh, ot) in enumerate(HEADS):
        query[h] = keep_half(proj[here, tile(qt)] * SCALE, qh)
        upstream[h] = keep_half(mixed_grad[:, tile(ot)], vh)
    for pair in range(2):
        product = (mixed[:, tile(pair)].astype(f32) * mixed_grad[:, tile(pair)].astype(f32)).T
        if pair == 0:
            row_dot[0:1, :] = jnp.sum(product[:HD], axis=0, keepdims=True)
            row_dot[1:2, :] = jnp.sum(product[HD:], axis=0, keepdims=True)
        else:
            row_dot[2:3, :] = jnp.sum(product[HD:], axis=0, keepdims=True)

    def body(kb, carry):
        at = pl.multiple_of(kb * block, block)
        keys = pl.ds(at, block)
        bias = document_bias(seg_col, seg_row, at, block)
        for h, (_, kt, _, vt, _, _) in enumerate(HEADS):
            key_tile, value_tile = proj[keys, tile(kt)], proj[keys, tile(vt)]
            prob = jnp.exp(mm_nt(key_tile, query[h]) + bias - lse[h : h + 1, :])
            prob_grad = mm_nt(value_tile, upstream[h])
            score_grad = (prob * (prob_grad - row_dot[h : h + 1, :])).astype(bf16)
            grad_acc[keys, tile(vt)] += mm(prob.astype(bf16), upstream[h])
            grad_acc[keys, tile(kt)] += mm(score_grad, query[h])
            query_acc[h] += mm_tn(key_tile, score_grad)
        return carry

    lax.fori_loop(low, high, body, 0)
    query_grads = [
        (query_acc[h, qh * HD : (qh + 1) * HD, :] * SCALE) for h, (_, _, qh, _, _, _) in enumerate(HEADS)
    ]
    first = jnp.concatenate(query_grads[:2], axis=0).T
    second = jnp.concatenate([query_grads[2], jnp.zeros_like(query_grads[2])], axis=0).T
    grad_acc[here, tile(0)] = first
    grad_acc[here, tile(3)] = second
    bias_ref[:, tile(0)] += fold(first, jnp.add)
    bias_ref[:, tile(4)] += fold(second, jnp.add)

    @pl.when(step == pl.num_programs(0) - 1)
    def _():
        grad_ref[:, tile(0)] = grad_acc[:, tile(0)].astype(bf16)
        grad_ref[:, tile(1)] = grad_acc[:, tile(1)].astype(bf16)
        grad_ref[:, tile(2)] = grad_acc[:, tile(2)].astype(bf16)
        grad_ref[:, tile(3)] = jnp.zeros_like(grad_ref[:, tile(3)])
        grad_ref[:, tile(4)] = (grad_acc[:, tile(4)] + grad_acc[:, tile(3)]).astype(bf16)
        grad_ref[:, tile(5)] = grad_acc[:, tile(5)].astype(bf16)
        bias_ref[:, tile(2)] += fold(grad_acc[:, tile(2)], jnp.add)
        bias_ref[:, tile(4)] += fold(grad_acc[:, tile(4)], jnp.add)


def attend_back(proj, segment, mixed, lse, mixed_grad, rows=512, block=256):
    length, cols = proj.shape
    count = 3
    whole = lambda width: pl.BlockSpec((length, width), lambda i, b: (0, 0))
    part = lambda width: pl.BlockSpec((rows, width), lambda i, b: (i, 0))
    row = lambda height: pl.BlockSpec((height, rows), lambda i, b: (0, i))
    grad, bias = pl.pallas_call(
        functools.partial(attend_back_kernel, block),
        grid_spec=pltpu.PrefetchScalarGridSpec(
            num_scalar_prefetch=1,
            grid=(length // rows,),
            in_specs=[
                whole(cols),
                whole(1),
                row(1),
                part(2 * TILE),
                row(8),
                part(2 * TILE),
            ],
            out_specs=[whole(cols), pl.BlockSpec((8, cols), lambda i, b: (0, 0))],
            scratch_shapes=[
                pltpu.VMEM((length, cols), f32),
                pltpu.VMEM((count, TILE, rows), f32),
                pltpu.VMEM((count, rows, TILE), bf16),
                pltpu.VMEM((count, rows, TILE), bf16),
                pltpu.VMEM((8, rows), f32),
            ],
        ),
        out_shape=[
            jax.ShapeDtypeStruct((length, cols), bf16),
            jax.ShapeDtypeStruct((8, cols), f32),
        ],
        compiler_params=pltpu.CompilerParams(vmem_limit_bytes=48 << 20),
        cost_estimate=pl.CostEstimate(
            flops=1_000_000_000, transcendentals=length * length * 3 // 2, bytes_accessed=8 << 20
        ),
        name="attend_back",
    )(
        document_blocks(segment, rows, block),
        proj,
        segment[:, None],
        segment[None, :],
        mixed,
        lse,
        mixed_grad,
    )
    return grad, jnp.sum(bias, axis=0)


def to_tiles(query, key, value, out):
    cut = lambda part, begin, end: part[..., begin:end]
    return jnp.concatenate(
        [cut(part, 0, TILE) for part in (query, key, value, out)]
        + [cut(part, TILE, TILE + HD) for part in (query, value, key, out)],
        axis=-1,
    )


def from_tiles(tiles):
    join = lambda first, last: jnp.concatenate(
        [tiles[..., tile(first)], tiles[..., last * HD : (last + 1) * HD]], axis=-1
    )
    return join(0, 8), join(1, 10), join(2, 9), join(3, 11)


def shards(
    tokens,
    segments,
    query_weight,
    query_bias,
    key_weight,
    value_weight,
    value_bias,
    out_weight,
    out_bias,
    attn_gain,
    attn_shift,
    inner_weight,
    inner_bias,
    outer_weight,
    outer_bias,
    ffn_gain,
    ffn_shift,
    out_grad,
):
    share, width = tokens.shape
    rows, head_width = query_weight.shape
    y, core = lax.axis_index("y"), lax.axis_index("c")
    start = core * share
    other_start = (1 - core) * share

    def own_rows(full):
        return lax.dynamic_slice_in_dim(full, start, share, 0)

    def other_rows(full):
        return lax.dynamic_slice_in_dim(full, other_start, share, 0)

    def ordered(own, other):
        return jnp.where(core == 0, jnp.concatenate([own, other]), jnp.concatenate([other, own]))

    def whole(own):
        return ordered(own, swap(own, "c"))

    def pair_sum(product):
        sent = swap(product(other_rows).astype(bf16), "c")
        return product(own_rows) + sent.astype(f32)

    head_block = to_tiles(
        *(part.astype(bf16) for part in (query_weight, key_weight, value_weight, out_weight))
    )
    head_parts = line_parts(head_block)
    outer_pair = after(outer_weight.astype(bf16), head_block)
    outer_pair = in_order(lax.axis_index("x"), outer_pair, swap(outer_pair, "x"), 0)
    outer_far = swap(outer_pair, "y")
    segment = pick(segments, y, 0)
    no_bias = jnp.zeros_like(query_bias)
    biases = jnp.concatenate([to_tiles(query_bias, no_bias, value_bias, no_bias), inner_bias])
    far_biases = swap(biases, "y")
    full_tokens = whole(tokens)
    head_line = line_order(all_after(head_parts, full_tokens, far_biases, outer_pair))
    head_one = spread_first(head_line)
    inner_parts = line_parts(after(inner_weight.astype(bf16), head_line))
    outer_plane = jnp.stack([outer_pair, after(outer_far, *head_one)])
    outer_line = line_parts(outer_plane)
    head_two = spread_second(*head_one)
    inner_line = line_order(all_after(inner_parts, *head_two))
    inner_one = spread_first(inner_line)
    head_own, head_far = spread_end(*head_one, *head_two)

    cols = 4 * head_width
    proj_own = (mm(full_tokens, head_own) + biases[:cols]).astype(bf16)
    proj_far = (mm(full_tokens, head_far) + far_biases[:cols]).astype(bf16)
    inner_one = [*inner_one[:2], *all_after(inner_one[2:], proj_own, proj_far)]
    inner_two = spread_second(*inner_one)
    proj_own = after(proj_own, *inner_one)

    (mixed_own, mixed_far), log_totals = attend_forward((proj_own, proj_far), segment)
    out_mats = [jnp.concatenate([mat[:, tile(3)], mat[:, tile(5)]], axis=1) for mat in (head_own, head_far)]
    attn_total = pair_sum(
        lambda take: mm_nt(take(mixed_own), out_mats[0]) + mm_nt(take(mixed_far), out_mats[1])
    )
    hidden, normed_one, inv_one = normalize_rows(
        tokens.astype(f32) + attn_total + out_bias, attn_gain, attn_shift
    )
    hidden_low = whole(hidden.astype(bf16))
    inner_mats = spread_end(*inner_one, *(after(part, hidden) for part in inner_two))

    actives, slopes = [], []
    for mat, bias in zip(inner_mats, (biases[cols:], far_biases[cols:])):
        inner_pre = mm(hidden_low, mat) + bias
        cdf = phi_cdf(inner_pre)
        actives.append((inner_pre * cdf).astype(bf16))
        slopes.append(cdf + inner_pre * jnp.exp(-0.5 * inner_pre * inner_pre) * INV_ROOT_TAU)
    outer_mats = plane_end(line_order(all_after(outer_line, *actives)))
    ffn_total = pair_sum(
        lambda take: mm_nt(take(actives[0]), outer_mats[0]) + mm_nt(take(actives[1]), outer_mats[1])
    )
    out_full, normed_two, inv_two = normalize_rows(
        hidden + ffn_total + outer_bias, ffn_gain, ffn_shift
    )
    layer_out = out_full.astype(bf16)
    grad_two, ffn_gain_part, ffn_shift_part = normalize_back(
        out_grad.astype(f32), normed_two, inv_two, ffn_gain
    )
    grad_two_low = whole(grad_two.astype(bf16))

    lines = lax.axis_size("z")
    outer_grads = jnp.stack(
        [mm_tn(grad_two_low, active).reshape(lines, 2, rows, width) for active in actives], axis=1
    )
    outer_parts = line_sum(outer_grads)
    grad_two_low = after(grad_two_low, outer_grads)
    inner_grads = [mm(grad_two_low, mat) * slope for mat, slope in zip(outer_mats, slopes)]
    inner_bias_parts = [jnp.sum(grad, axis=0) for grad in inner_grads]
    inner_lows = [grad.astype(bf16) for grad in inner_grads]
    back_total = pair_sum(
        lambda take: mm_nt(take(inner_lows[0]), inner_mats[0])
        + mm_nt(take(inner_lows[1]), inner_mats[1])
    )
    inner_got = collect_first(*(mm_tn(hidden_low, low) for low in inner_lows), rows)
    grad_one, attn_gain_part, attn_shift_part = normalize_back(
        grad_two + back_total, normed_one, inv_one, attn_gain
    )
    row_sums = jnp.stack(
        [
            jnp.sum(grad_one, axis=0),
            attn_gain_part,
            attn_shift_part,
            jnp.sum(grad_two, axis=0),
            ffn_gain_part,
            ffn_shift_part,
        ]
    )
    grad_one_block = jnp.concatenate([grad_one.astype(bf16), split_low(row_sums)])
    other_block = swap(grad_one_block, "c")
    grad_one_low = ordered(grad_one_block[:share], other_block[:share])
    row_sums = row_sums + join_low(other_block[share:])
    mixed_grads = [mm(grad_one_low, mat).astype(bf16) for mat in out_mats]
    grad_far, bias_far = attend_back(
        proj_far, segment, mixed_far, log_totals[8:], mixed_grads[1]
    )

    def head_grad(grad, mixed):
        out_grad_tiles = mm_tn(grad_one_low, mixed)
        tiles = mm_tn(full_tokens, grad)
        return jnp.concatenate(
            [
                tiles[:, : 3 * TILE],
                out_grad_tiles[:, :TILE],
                tiles[:, tile(4)],
                tiles[:, tile(5)] + out_grad_tiles[:, TILE:],
            ],
            axis=1,
        )

    far_rows = jnp.concatenate([jnp.stack([bias_far, inner_bias_parts[1]]), row_sums])
    far_block = jnp.concatenate(
        [head_grad(grad_far, mixed_far).astype(bf16), split_low(far_rows)]
    )
    far_got = swap(far_block, "y")
    inner_more = collect_second(*inner_got[:2], *(after(part, grad_far) for part in inner_got[2:]))
    proj_own_late = after(proj_own, far_block)
    grad_own, bias_own = attend_back(
        proj_own_late, segment, mixed_own, log_totals[:8], mixed_grads[0]
    )
    outer_parts = [outer_parts[0], *(after(part, grad_own) for part in outer_parts[1:])]
    inner_more = [*inner_more[:2], *(after(part, grad_own) for part in inner_more[2:])]
    far_got = after(far_got, grad_own)
    inner_parts = line_sum(collect_third(*inner_more))

    x = lax.axis_index("x")
    head = (head_grad(grad_own, mixed_own) + far_got[:width].astype(f32)).reshape(lines, 2, rows, width)
    own_rows_now = jnp.concatenate([jnp.stack([bias_own, inner_bias_parts[0]]), row_sums]) + join_low(
        far_got[width:]
    )
    head_sent = swap(
        jnp.concatenate(
            [pick(head, 1 - x, 1).reshape(-1, width).astype(bf16), split_low(own_rows_now)]
        ),
        "x",
    )
    outer_two = add_all(outer_parts)
    outer_x = pick(outer_two, x, 1) + swap(pick(outer_two, 1 - x, 1).astype(bf16), "x").astype(f32)
    input_total = pair_sum(
        lambda take: mm_nt(take(grad_own), head_own) + mm_nt(take(grad_far), head_far)
    )
    tokens_grad = grad_one + input_total
    outer_sum = outer_x[0] + swap(outer_x[1].astype(bf16), "y").astype(f32)
    inner_sum = add_all(inner_parts)
    head = pick(head, x, 1) + head_sent[: lines * rows].reshape(lines, rows, width).astype(f32)
    own_rows_now = own_rows_now + join_low(head_sent[lines * rows :])
    if lines > 4:
        head_sum, sums = lax.psum_scatter(head, "z", scatter_dimension=0), lax.psum(own_rows_now, "z")
    else:
        z = lax.axis_index("z")
        low_rows = split_low(own_rows_now)
        head_sum, sums = pick(head, z, 0), own_rows_now
        for k in range(1, lines):
            sent = shift(
                jnp.concatenate([pick(head, lax.rem(z + k, lines), 0).astype(bf16), low_rows]), "z", k
            )
            head_sum = head_sum + sent[:rows].astype(f32)
            sums = sums + join_low(sent[rows:])
    query_bias_grad, _, value_bias_grad, _ = from_tiles(sums[0])
    query_wsum, key_wsum, value_wsum, out_wsum = from_tiles(head_sum)
    return (
        layer_out,
        tokens_grad,
        query_wsum,
        query_bias_grad,
        key_wsum,
        value_wsum,
        value_bias_grad,
        out_wsum,
        sums[2],
        sums[3],
        sums[4],
        inner_sum,
        sums[1],
        outer_sum,
        sums[5],
        sums[6],
        sums[7],
    )


def solution(mesh):
    groups, tensor = mesh.shape["dp"], mesh.shape["tensor"]
    grid = Mesh(mesh.devices.reshape(groups // 2, 2, tensor // 2, 2), ("z", "x", "y", "c"))
    dp, tp = ("z", "x"), ("y", "c")
    every = ("z", "x", "y", "c")
    by_row, none, flat, both = P(every, None), P(), P(tp), P(dp, tp)
    in_specs = (
        by_row,
        P(dp, None),
        both,
        flat,
        both,
        both,
        flat,
        both,
        none,
        none,
        none,
        both,
        flat,
        both,
        none,
        none,
        none,
        by_row,
    )
    out_specs = (
        by_row,
        by_row,
        both,
        flat,
        both,
        both,
        flat,
        both,
        none,
        none,
        none,
        both,
        flat,
        both,
        none,
        none,
        none,
    )
    return jax.shard_map(shards, mesh=grid, in_specs=in_specs, out_specs=out_specs, check_vma=False)
```
